32 devices in a mesh: grp: 2 (over x), row: 16 (over z, y, core).
Axes of the slice: x: 2, y: 2, z: 4, core: 2. Of those that a mesh axis runs over, the one named last changes fastest.
Arguments:
- slc: bfloat16 [2, 300, 64, 256], P(None, None, ('grp', 'row')), parts along dimension 2, may hold values from -8 to 8
- mask: int32 [25, 64, 256], P(None, ('grp', 'row')), parts along dimension 1, may hold values 0 or 1
- ref_index: int32 [2], P('grp'), parts along dimension 0, may hold values from 0 to 8191
Outputs:
- linked: float32 [2, 300, 64, 256], P(None, None, ('grp', 'row')), parts along dimension 2
The draws below stay inside these ranges and needn't reach their ends.
There are 2 independent parts, one for each index of `grp`. The reference program is written for one: setup_inputs(seed, part) draws one part's arguments, and reference() takes and returns one part's arrays. A program takes and returns all parts, laid end to end along the dimension named above; each array names one. Nothing has to cross between parts.
All inputs are finite; a program needn't handle non-finite values. No bound on the sum of `mask` on one device may be relied on, other than what follows from the above.
Results may differ from the reference program's by a relative error of at most 0.0046.
Values may be sent and summed in bfloat16 or wider, within the bound.
A program may use at most 64 MiB of HBM per device.

```python
import math
import jax
import jax.numpy as jnp
from jax import lax

NDATE = 300
NC = 256
HALF = 2
ITERS = 2
OFFS = 25
NR = 32


def draw_slc(key, part):
    first, second, third = jax.random.split(key, 3)
    noise = jax.random.normal(first, (2, NDATE, NR, NC), jnp.float32)
    logamp = jax.random.uniform(second, (1, NDATE, NR, 1), jnp.float32, math.log(0.5), math.log(2.0))
    field = noise
    return jnp.clip(jnp.exp(logamp) * field, -8.0, 8.0).astype(jnp.bfloat16)


def with_ends(drawn, stream_key, smallest, high):
    longest = drawn.shape.index(max(drawn.shape))
    spots = []
    for shift in (0, 1):
        where = [jax.random.randint(jax.random.fold_in(stream_key, axis), (), 0, length) for axis, length in enumerate(drawn.shape)]
        where[longest] = (where[longest] + shift) % drawn.shape[longest]
        spots.append(tuple(where))
    return drawn.at[spots[0]].set(smallest).at[spots[1]].set(high)


def setup_inputs(seed: int = 0, part: int = 0) -> dict:
    keys = jax.random.split(jax.random.key(seed), 4)
    part_splits = jax.random.split(jax.random.fold_in(keys[3], part), 4)
    return {
        "slc": draw_slc(jax.random.fold_in(jax.random.fold_in(keys[3], part), 71), part),
        "mask": with_ends((jax.random.randint(part_splits[1], (OFFS, NR, NC), 0, 2) < 1).astype(jnp.int32), jax.random.fold_in(part_splits[1], 1), 0, 1),
        "ref_index": jax.random.randint(part_splits[2], (1,), 0, NR * NC).astype(jnp.int32),
    }


def link_pixels(extended, mask, total_rows):
    rows = extended.shape[2] - 2 * HALF
    cols = extended.shape[3]
    padded = jnp.pad(extended, ((0, 0), (0, 0), (0, 0), (HALF, HALF)))
    row_ids = jnp.arange(rows)[:, None]
    col_ids = jnp.arange(cols)[None, :]
    width = 2 * HALF + 1
    weights = []
    count = jnp.zeros((rows, cols), jnp.float32)
    for row_shift in range(-HALF, HALF + 1):
        for col_shift in range(-HALF, HALF + 1):
            offset = (row_shift + HALF) * width + col_shift + HALF
            inside = (row_ids + row_shift >= 0) & (row_ids + row_shift < total_rows)
            inside = inside & (col_ids + col_shift >= 0) & (col_ids + col_shift < cols)
            if row_shift == 0 and col_shift == 0:
                chosen = inside
            else:
                chosen = inside & (mask[offset] == 1)
            weight = chosen.astype(jnp.float32)
            weights.append(weight)
            count = count + weight
    inverse = 1.0 / count
    vector = padded[:, :, HALF:HALF + rows, HALF:HALF + cols].astype(jnp.float32)
    for step in range(ITERS):
        total_real = jnp.zeros((NDATE, rows, cols), jnp.float32)
        total_imag = jnp.zeros((NDATE, rows, cols), jnp.float32)
        for row_shift in range(-HALF, HALF + 1):
            for col_shift in range(-HALF, HALF + 1):
                offset = (row_shift + HALF) * width + col_shift + HALF
                piece = padded[:, :, HALF + row_shift:HALF + row_shift + rows, HALF + col_shift:HALF + col_shift + cols].astype(jnp.float32)
                proj_real = lax.optimization_barrier(jnp.sum(piece[0] * vector[0] + piece[1] * vector[1], axis=0)) / NDATE
                proj_imag = lax.optimization_barrier(jnp.sum(piece[0] * vector[1] - piece[1] * vector[0], axis=0)) / NDATE
                coef_real = weights[offset] * inverse * proj_real
                coef_imag = weights[offset] * inverse * proj_imag
                total_real = total_real + coef_real * piece[0] - coef_imag * piece[1]
                total_imag = total_imag + coef_real * piece[1] + coef_imag * piece[0]
        factor = lax.rsqrt(lax.optimization_barrier(jnp.mean(total_real * total_real + total_imag * total_imag, axis=0)) + 0.001)
        vector = jnp.stack([total_real * factor, total_imag * factor])
    return vector

def reference(slc, mask, ref_index):
    row_count = slc.shape[2]
    col_count = slc.shape[3]
    data = slc.astype(jnp.float32)
    power = lax.optimization_barrier(jnp.sum(data[0] * data[0] + data[1] * data[1], axis=(1, 2)))
    gains = lax.rsqrt(power / (row_count * col_count) + 0.1)
    scaled = (data * gains[:, None, None]).astype(jnp.bfloat16)
    extended = jnp.pad(scaled, ((0, 0), (0, 0), (HALF, HALF), (0, 0)))
    vector = link_pixels(extended, mask, row_count)
    target = ref_index[0].astype(jnp.int32)
    row_target = (target // col_count).astype(jnp.int32)
    col_target = (target % col_count).astype(jnp.int32)
    zero = jnp.zeros((), jnp.int32)
    picked = lax.dynamic_slice(vector, (zero, zero, row_target, col_target), (2, NDATE, 1, 1))
    real_ref = picked[0]
    imag_ref = picked[1]
    out_real = vector[0] * real_ref + vector[1] * imag_ref
    out_imag = vector[1] * real_ref - vector[0] * imag_ref
    return jnp.stack([out_real, out_imag])
```

```python
import jax
import jax.numpy as jnp
from jax import lax
from jax.experimental import pallas as pl
from jax.experimental.pallas import tpu as pltpu
from jax.sharding import PartitionSpec as P

HALF = 2
ITERS = 2
WIDTH = 2 * HALF + 1
LANE = 128
SUB = 16
MESH = pl.DeviceIdType.MESH


def round_up(value, unit):
    return (value + unit - 1) // unit * unit


def row_of(column_sums):
    return jnp.sum(column_sums.T, axis=0, keepdims=True)


def kernel(
    n, ndate, total_rows, x_ref, mask_ref, index_ref, out_ref,
    low, high, flat, turned, weight, coef, column, powers, refs,
    low_sem, high_sem, power_sem, ref_sem,
):
    rows, depth, cols = x_ref.shape
    half_depth = depth // 2
    blocks = cols // LANE
    long_dates = powers.shape[2]
    long_depth = refs.shape[2]
    me = lax.axis_index("row")
    first_row = me * rows

    def peer(k):
        return lax.rem(me + k, n)

    barrier = pltpu.get_barrier_semaphore()

    @pl.loop(1, n)
    def _(k):
        pl.semaphore_signal(barrier, inc=1, device_id={"row": peer(k)}, device_id_type=MESH)

    column[...] = jnp.zeros_like(column)
    sums = jnp.zeros((half_depth, LANE), jnp.float32)
    for r in range(rows):
        for part in range(2):
            for block in range(blocks):
                piece = x_ref[r, part * half_depth:(part + 1) * half_depth, block * LANE:(block + 1) * LANE]
                piece = piece.astype(jnp.float32)
                sums = sums + piece * piece
    column[0:half_depth, :] = sums
    powers[me] = row_of(column[0:long_dates, :])

    pl.semaphore_wait(barrier, n - 1)

    def exchange(buffer, sems):
        def copy(k, slot):
            return pltpu.make_async_remote_copy(
                src_ref=buffer.at[slot], dst_ref=buffer.at[slot],
                send_sem=sems.at[0, k], recv_sem=sems.at[1, slot],
                device_id={"row": peer(k)}, device_id_type=MESH,
            )

        def start():
            @pl.loop(1, n)
            def _(k):
                copy(k, me).start()

        def finish():
            @pl.loop(1, n)
            def _(k):
                copy(k, peer(k)).wait_recv()

            @pl.loop(1, n)
            def _(k):
                copy(k, me).wait_send()

        return start, finish

    start_power, finish_power = exchange(powers, power_sem)
    start_ref, finish_ref = exchange(refs, ref_sem)
    start_power()

    up = pltpu.make_async_remote_copy(
        src_ref=x_ref.at[rows - HALF:rows], dst_ref=low, send_sem=low_sem.at[0], recv_sem=low_sem.at[1],
        device_id={"row": jnp.minimum(me + 1, n - 1)}, device_id_type=MESH,
    )
    down = pltpu.make_async_remote_copy(
        src_ref=x_ref.at[0:HALF], dst_ref=high, send_sem=high_sem.at[0], recv_sem=high_sem.at[1],
        device_id={"row": jnp.maximum(me - 1, 0)}, device_id_type=MESH,
    )
    has_next = me < n - 1
    has_prev = me > 0
    pl.when(has_next)(up.start)
    pl.when(has_prev)(down.start)

    @pl.when(me == 0)
    def _():
        low[...] = jnp.zeros_like(low)

    @pl.when(me == n - 1)
    def _():
        high[...] = jnp.zeros_like(high)

    row_ids = first_row + lax.broadcasted_iota(jnp.int32, (rows, cols), 0)
    col_ids = lax.broadcasted_iota(jnp.int32, (rows, cols), 1)
    chosen = []
    count = jnp.zeros((rows, cols), jnp.float32)
    for a in range(-HALF, HALF + 1):
        for b in range(-HALF, HALF + 1):
            inside = (row_ids + a >= 0) & (row_ids + a < total_rows)
            inside = inside & (col_ids + b >= 0) & (col_ids + b < cols)
            if (a, b) != (0, 0):
                inside = inside & (mask_ref[(a + HALF) * WIDTH + b + HALF] == 1)
            one = inside.astype(jnp.float32)
            chosen.append(one)
            count = count + one
    inverse = 1.0 / (count * ndate)

    def window(block):
        return max(0, block * LANE - SUB), min(cols, (block + 1) * LANE + SUB)

    coef[...] = jnp.zeros_like(coef)
    for block in range(blocks):
        begin, end = window(block)
        shape = (end - begin, LANE)
        shift = begin - block * LANE
        shift = shift + lax.broadcasted_iota(jnp.int32, shape, 0) - lax.broadcasted_iota(jnp.int32, shape, 1)
        for r in range(rows):
            for a in range(WIDTH):
                band = jnp.zeros(shape, jnp.float32)
                for b in range(WIDTH):
                    line = (chosen[a * WIDTH + b] * inverse)[r:r + 1, block * LANE:(block + 1) * LANE]
                    band = jnp.where(shift == b - HALF, line, band)
                weight[block, r, a, 0:end - begin, :] = band

    finish_power()
    power = jnp.sum(powers[...], axis=0)
    gain_row = lax.rsqrt(power * (1.0 / (total_rows * cols)) + 0.1)
    gain = jnp.broadcast_to(gain_row, (LANE, long_dates)).T[0:half_depth, :]
    gain = jnp.concatenate([gain] * blocks, axis=1)
    turned[...] = jnp.zeros_like(turned)

    def calibrate(source, place):
        for part in range(2):
            rows_here = slice(part * half_depth, (part + 1) * half_depth)
            scaled = (source[rows_here, :].astype(jnp.float32) * gain).astype(jnp.bfloat16)
            flat[rows_here, place * cols:(place + 1) * cols] = scaled
        turned[place] = flat[:, place * cols:(place + 1) * cols].T

    flat[...] = jnp.zeros_like(flat)
    for r in range(rows):
        calibrate(x_ref.at[r], r + HALF)

    @pl.when(has_prev)
    def _():
        up.wait_recv()

    @pl.when(has_next)
    def _():
        down.wait_recv()

    for r in range(HALF):
        calibrate(low.at[r], r)
        calibrate(high.at[r], r + HALF + rows)

    target = index_ref[0]
    picked = jnp.zeros((depth, LANE), jnp.float32)
    for r in range(rows):
        for block in range(blocks):
            begin, end = window(block)
            lanes = slice((r + HALF) * cols + block * LANE, (r + HALF) * cols + (block + 1) * LANE)
            real = flat[0:half_depth, lanes]
            imag = flat[half_depth:depth, lanes]
            for step in range(ITERS):
                pair = jnp.concatenate(
                    [jnp.concatenate([real, imag], axis=1), jnp.concatenate([imag, -real], axis=1)], axis=0
                )
                for a in range(WIDTH):
                    proj = jnp.dot(
                        turned[r + a, begin:end, 0:depth], pair, preferred_element_type=jnp.float32
                    )
                    band = weight[block, r, a, 0:end - begin, :]
                    both = jnp.concatenate([band, band], axis=1)
                    coef[block, a * cols + begin:a * cols + end, :] = (proj * both).astype(jnp.bfloat16)
                product = jnp.dot(
                    flat[0:depth, r * cols:(r + WIDTH) * cols], coef[block], preferred_element_type=jnp.float32
                )
                top, bottom = product[0:half_depth], product[half_depth:depth]
                new_real = top[:, 0:LANE] - bottom[:, LANE:2 * LANE]
                new_imag = top[:, LANE:2 * LANE] + bottom[:, 0:LANE]
                energy = jnp.sum(new_real * new_real + new_imag * new_imag, axis=0, keepdims=True)
                factor = lax.rsqrt(energy * (1.0 / ndate) + 0.001)
                new_real = new_real * factor
                new_imag = new_imag * factor
                real = new_real.astype(jnp.bfloat16)
                imag = new_imag.astype(jnp.bfloat16)
            lanes = slice(block * LANE, (block + 1) * LANE)
            out_ref[r, 0:half_depth, lanes] = new_real
            out_ref[r, half_depth:depth, lanes] = new_imag
            place = (first_row + r) * cols + block * LANE + lax.broadcasted_iota(jnp.int32, (1, LANE), 1)
            here = place == target
            picked = picked + jnp.concatenate(
                [jnp.where(here, new_real, 0.0), jnp.where(here, new_imag, 0.0)], axis=0
            )

    column[...] = jnp.zeros_like(column)
    column[0:depth, :] = picked
    refs[me] = row_of(column[...])
    start_ref()
    finish_ref()
    refvec = jnp.sum(refs[...], axis=0)
    refvec = jnp.broadcast_to(refvec, (LANE, long_depth)).T
    ref_real = refvec[0:half_depth]
    ref_imag = refvec[half_depth:depth]
    for r in range(rows):
        for block in range(blocks):
            lanes = slice(block * LANE, (block + 1) * LANE)
            real = out_ref[r, 0:half_depth, lanes]
            imag = out_ref[r, half_depth:depth, lanes]
            out_ref[r, 0:half_depth, lanes] = real * ref_real + imag * ref_imag
            out_ref[r, half_depth:depth, lanes] = imag * ref_real - real * ref_imag

    pl.when(has_next)(up.wait_send)
    pl.when(has_prev)(down.wait_send)


def per_device(slc, mask, ref_index):
    parts, ndate, rows, cols = slc.shape
    n = lax.axis_size("row")
    half_depth = round_up(ndate, SUB)
    depth = 2 * half_depth
    long_dates = round_up(half_depth, LANE)
    long_depth = round_up(depth, LANE)
    blocks = cols // LANE
    span = rows + 2 * HALF
    x = jnp.pad(slc.transpose(2, 0, 1, 3), ((0, 0), (0, 0), (0, half_depth - ndate), (0, 0)))
    x = x.reshape(rows, depth, cols)
    vmem = pl.BlockSpec(memory_space=pltpu.VMEM)

    def body(*refs):
        kernel(n, ndate, rows * n, *refs)

    out = pl.pallas_call(
        body,
        out_shape=jax.ShapeDtypeStruct((rows, depth, cols), jnp.float32),
        in_specs=[vmem, vmem, pl.BlockSpec(memory_space=pltpu.SMEM)],
        out_specs=vmem,
        scratch_shapes=[
            pltpu.VMEM((HALF, depth, cols), jnp.bfloat16),
            pltpu.VMEM((HALF, depth, cols), jnp.bfloat16),
            pltpu.VMEM((long_depth, span * cols), jnp.bfloat16),
            pltpu.VMEM((span, cols, long_depth), jnp.bfloat16),
            pltpu.VMEM((blocks, rows, WIDTH, LANE + 2 * SUB, LANE), jnp.float32),
            pltpu.VMEM((blocks, WIDTH * cols, 2 * LANE), jnp.bfloat16),
            pltpu.VMEM((long_depth, LANE), jnp.float32),
            pltpu.VMEM((n, 1, long_dates), jnp.float32),
            pltpu.VMEM((n, 1, long_depth), jnp.float32),
            pltpu.SemaphoreType.DMA((2,)),
            pltpu.SemaphoreType.DMA((2,)),
            pltpu.SemaphoreType.DMA((2, n)),
            pltpu.SemaphoreType.DMA((2, n)),
        ],
        compiler_params=pltpu.CompilerParams(collective_id=0, has_side_effects=True),
        name="link",
    )(x, mask, ref_index)
    out = out.reshape(rows, parts, half_depth, cols)[:, :, :ndate]
    return out.transpose(1, 2, 0, 3)


def solution(mesh):
    placed = (P(None, None, ("grp", "row"), None), P(None, ("grp", "row"), None), P("grp"))
    return jax.shard_map(
        per_device,
        mesh=mesh,
        in_specs=placed,
        out_specs=P(None, None, ("grp", "row"), None),
        check_vma=False,
    )
```

```python
import jax
import jax.numpy as jnp
from jax import lax
from jax.experimental import pallas as pl
from jax.experimental.pallas import tpu as pltpu
from jax.sharding import PartitionSpec as P

HALF = 2
ITERS = 2
WIDTH = 2 * HALF + 1
LANE = 128
SUB = 16
MESH = pl.DeviceIdType.MESH


def round_up(value, unit):
    return (value + unit - 1) // unit * unit


def row_of(column_sums):
    return jnp.sum(column_sums.T, axis=0, keepdims=True)


def kernel(
    n, ndate, total_rows, x_ref, mask_ref, index_ref, out_ref,
    low, high, flat, turned, weight, coef, column, powers, refs,
    low_sem, high_sem, power_sem, ref_sem,
):
    rows, _, _, cols = x_ref.shape
    half_depth = out_ref.shape[1] // 2
    depth = 2 * half_depth
    blocks = cols // LANE
    long_dates = powers.shape[2]
    long_depth = refs.shape[2]
    me = lax.axis_index("row")
    first_row = me * rows

    def peer(k):
        return lax.rem(me + k, n)

    barrier = pltpu.get_barrier_semaphore()

    @pl.loop(1, n)
    def _(k):
        pl.semaphore_signal(barrier, inc=1, device_id={"row": peer(k)}, device_id_type=MESH)

    pl.semaphore_wait(barrier, n - 1)

    def exchange(buffer, sems):
        def copy(k, slot):
            return pltpu.make_async_remote_copy(
                src_ref=buffer.at[slot], dst_ref=buffer.at[slot],
                send_sem=sems.at[0, k], recv_sem=sems.at[1, slot],
                device_id={"row": peer(k)}, device_id_type=MESH,
            )

        def start():
            @pl.loop(1, n)
            def _(k):
                copy(k, me).start()

        def finish():
            @pl.loop(1, n)
            def _(k):
                copy(k, peer(k)).wait_recv()

            @pl.loop(1, n)
            def _(k):
                copy(k, me).wait_send()

        return start, finish

    start_power, finish_power = exchange(powers, power_sem)
    start_ref, finish_ref = exchange(refs, ref_sem)

    up = pltpu.make_async_remote_copy(
        src_ref=x_ref.at[rows - HALF:rows], dst_ref=low, send_sem=low_sem.at[0], recv_sem=low_sem.at[1],
        device_id={"row": jnp.minimum(me + 1, n - 1)}, device_id_type=MESH,
    )
    down = pltpu.make_async_remote_copy(
        src_ref=x_ref.at[0:HALF], dst_ref=high, send_sem=high_sem.at[0], recv_sem=high_sem.at[1],
        device_id={"row": jnp.maximum(me - 1, 0)}, device_id_type=MESH,
    )
    has_next = me < n - 1
    has_prev = me > 0
    pl.when(has_next)(up.start)
    pl.when(has_prev)(down.start)

    column[...] = jnp.zeros_like(column)
    sums = jnp.zeros((ndate, LANE), jnp.float32)
    for r in range(rows):
        for part in range(2):
            for block in range(blocks):
                piece = x_ref[r, part, :, block * LANE:(block + 1) * LANE]
                piece = piece.astype(jnp.float32)
                sums = sums + piece * piece
    column[0:ndate, :] = sums
    powers[me] = row_of(column[0:long_dates, :])

    start_power()

    @pl.when(me == 0)
    def _():
        low[...] = jnp.zeros_like(low)

    @pl.when(me == n - 1)
    def _():
        high[...] = jnp.zeros_like(high)

    row_ids = first_row + lax.broadcasted_iota(jnp.int32, (rows, cols), 0)
    col_ids = lax.broadcasted_iota(jnp.int32, (rows, cols), 1)
    chosen = []
    count = jnp.zeros((rows, cols), jnp.float32)
    for a in range(-HALF, HALF + 1):
        for b in range(-HALF, HALF + 1):
            inside = (row_ids + a >= 0) & (row_ids + a < total_rows)
            inside = inside & (col_ids + b >= 0) & (col_ids + b < cols)
            if (a, b) != (0, 0):
                inside = inside & (mask_ref[(a + HALF) * WIDTH + b + HALF] == 1)
            one = inside.astype(jnp.float32)
            chosen.append(one)
            count = count + one
    inverse = 1.0 / (count * ndate)

    def window(block):
        return max(0, block * LANE - SUB), min(cols, (block + 1) * LANE + SUB)

    coef[...] = jnp.zeros_like(coef)
    for block in range(blocks):
        begin, end = window(block)
        shape = (end - begin, LANE)
        shift = begin - block * LANE
        shift = shift + lax.broadcasted_iota(jnp.int32, shape, 0) - lax.broadcasted_iota(jnp.int32, shape, 1)
        for r in range(rows):
            for a in range(WIDTH):
                band = jnp.zeros(shape, jnp.float32)
                for b in range(WIDTH):
                    line = (chosen[a * WIDTH + b] * inverse)[r:r + 1, block * LANE:(block + 1) * LANE]
                    band = jnp.where(shift == b - HALF, line, band)
                weight[block, r, a, 0:end - begin, :] = band

    finish_power()
    power = jnp.sum(powers[...], axis=0)
    gain_row = lax.rsqrt(power * (1.0 / (total_rows * cols)) + 0.1)
    gain = jnp.broadcast_to(gain_row, (LANE, long_dates)).T[0:ndate, :]
    gain = jnp.concatenate([gain] * blocks, axis=1)
    turned[...] = jnp.zeros_like(turned)

    def calibrate(source, place):
        for part in range(2):
            rows_here = slice(part * half_depth, part * half_depth + ndate)
            scaled = (source[part].astype(jnp.float32) * gain).astype(jnp.bfloat16)
            flat[rows_here, place * cols:(place + 1) * cols] = scaled
        turned[place] = flat[:, place * cols:(place + 1) * cols].T

    flat[...] = jnp.zeros_like(flat)
    for r in range(rows):
        calibrate(x_ref.at[r], r + HALF)

    @pl.when(has_prev)
    def _():
        up.wait_recv()

    @pl.when(has_next)
    def _():
        down.wait_recv()

    for r in range(HALF):
        calibrate(low.at[r], r)
        calibrate(high.at[r], r + HALF + rows)

    target = index_ref[0]
    picked = jnp.zeros((depth, LANE), jnp.float32)
    for r in range(rows):
        for block in range(blocks):
            begin, end = window(block)
            lanes = slice((r + HALF) * cols + block * LANE, (r + HALF) * cols + (block + 1) * LANE)
            real = flat[0:half_depth, lanes]
            imag = flat[half_depth:depth, lanes]
            for step in range(ITERS):
                pair = jnp.concatenate(
                    [jnp.concatenate([real, imag], axis=1), jnp.concatenate([imag, -real], axis=1)], axis=0
                )
                for a in range(WIDTH):
                    proj = jnp.dot(
                        turned[r + a, begin:end, 0:depth], pair, preferred_element_type=jnp.float32
                    )
                    band = weight[block, r, a, 0:end - begin, :]
                    both = jnp.concatenate([band, band], axis=1)
                    coef[block, a * cols + begin:a * cols + end, :] = (proj * both).astype(jnp.bfloat16)
                product = jnp.dot(
                    flat[0:depth, r * cols:(r + WIDTH) * cols], coef[block], preferred_element_type=jnp.float32
                )
                top, bottom = product[0:half_depth], product[half_depth:depth]
                new_real = top[:, 0:LANE] - bottom[:, LANE:2 * LANE]
                new_imag = top[:, LANE:2 * LANE] + bottom[:, 0:LANE]
                energy = jnp.sum(new_real * new_real + new_imag * new_imag, axis=0, keepdims=True)
                factor = lax.rsqrt(energy * (1.0 / ndate) + 0.001)
                new_real = new_real * factor
                new_imag = new_imag * factor
                real = new_real.astype(jnp.bfloat16)
                imag = new_imag.astype(jnp.bfloat16)
            lanes = slice(block * LANE, (block + 1) * LANE)
            out_ref[r, 0:half_depth, lanes] = new_real
            out_ref[r, half_depth:depth, lanes] = new_imag
            place = (first_row + r) * cols + block * LANE + lax.broadcasted_iota(jnp.int32, (1, LANE), 1)
            here = place == target
            picked = picked + jnp.concatenate(
                [jnp.where(here, new_real, 0.0), jnp.where(here, new_imag, 0.0)], axis=0
            )

    column[...] = jnp.zeros_like(column)
    column[0:depth, :] = picked
    refs[me] = row_of(column[...])
    start_ref()
    finish_ref()
    refvec = jnp.sum(refs[...], axis=0)
    refvec = jnp.broadcast_to(refvec, (LANE, long_depth)).T
    ref_real = refvec[0:half_depth]
    ref_imag = refvec[half_depth:depth]
    for r in range(rows):
        for block in range(blocks):
            lanes = slice(block * LANE, (block + 1) * LANE)
            real = out_ref[r, 0:half_depth, lanes]
            imag = out_ref[r, half_depth:depth, lanes]
            out_ref[r, 0:half_depth, lanes] = real * ref_real + imag * ref_imag
            out_ref[r, half_depth:depth, lanes] = imag * ref_real - real * ref_imag

    pl.when(has_next)(up.wait_send)
    pl.when(has_prev)(down.wait_send)


def per_device(slc, mask, ref_index):
    parts, ndate, rows, cols = slc.shape
    n = lax.axis_size("row")
    half_depth = round_up(ndate, SUB)
    depth = 2 * half_depth
    long_dates = round_up(half_depth, LANE)
    long_depth = round_up(depth, LANE)
    blocks = cols // LANE
    span = rows + 2 * HALF
    x = slc.transpose(2, 0, 1, 3)
    vmem = pl.BlockSpec(memory_space=pltpu.VMEM)

    def body(*refs):
        kernel(n, ndate, rows * n, *refs)

    out = pl.pallas_call(
        body,
        out_shape=jax.ShapeDtypeStruct((rows, depth, cols), jnp.float32),
        in_specs=[vmem, vmem, pl.BlockSpec(memory_space=pltpu.SMEM)],
        out_specs=vmem,
        scratch_shapes=[
            pltpu.VMEM((HALF, parts, ndate, cols), jnp.bfloat16),
            pltpu.VMEM((HALF, parts, ndate, cols), jnp.bfloat16),
            pltpu.VMEM((long_depth, span * cols), jnp.bfloat16),
            pltpu.VMEM((span, cols, long_depth), jnp.bfloat16),
            pltpu.VMEM((blocks, rows, WIDTH, LANE + 2 * SUB, LANE), jnp.float32),
            pltpu.VMEM((blocks, WIDTH * cols, 2 * LANE), jnp.bfloat16),
            pltpu.VMEM((long_depth, LANE), jnp.float32),
            pltpu.VMEM((n, 1, long_dates), jnp.float32),
            pltpu.VMEM((n, 1, long_depth), jnp.float32),
            pltpu.SemaphoreType.DMA((2,)),
            pltpu.SemaphoreType.DMA((2,)),
            pltpu.SemaphoreType.DMA((2, n)),
            pltpu.SemaphoreType.DMA((2, n)),
        ],
        compiler_params=pltpu.CompilerParams(collective_id=0, has_side_effects=True),
        name="link",
    )(x, mask, ref_index)
    out = out.reshape(rows, parts, half_depth, cols)[:, :, :ndate]
    return out.transpose(1, 2, 0, 3)


def solution(mesh):
    placed = (P(None, None, ("grp", "row"), None), P(None, ("grp", "row"), None), P("grp"))
    return jax.shard_map(
        per_device,
        mesh=mesh,
        in_specs=placed,
        out_specs=P(None, None, ("grp", "row"), None),
        check_vma=False,
    )
```

```python
import jax
import jax.numpy as jnp
from jax import lax
from jax.experimental import pallas as pl
from jax.experimental.pallas import tpu as pltpu
from jax.sharding import PartitionSpec as P

HALF = 2
ITERS = 2
WIDTH = 2 * HALF + 1
LANE = 128
SUB = 16
MESH = pl.DeviceIdType.MESH


def round_up(value, unit):
    return (value + unit - 1) // unit * unit


def row_of(column_sums):
    return jnp.sum(column_sums.T, axis=0, keepdims=True)


def kernel(
    n, ndate, total_rows, x_ref, mask_ref, index_ref, out_ref,
    low, high, flat, turned, weight, coef, total, column, powers, refs,
    low_sem, high_sem, power_sem, ref_sem,
):
    rows, depth, cols = x_ref.shape
    half_depth = depth // 2
    blocks = cols // LANE
    long_dates = powers.shape[2]
    long_depth = refs.shape[2]
    me = lax.axis_index("row")
    first_row = me * rows

    def peer(k):
        return lax.rem(me + k, n)

    barrier = pltpu.get_barrier_semaphore()

    @pl.loop(1, n)
    def _(k):
        pl.semaphore_signal(barrier, inc=1, device_id={"row": peer(k)}, device_id_type=MESH)

    column[...] = jnp.zeros_like(column)
    sums = jnp.zeros((half_depth, LANE), jnp.float32)
    for r in range(rows):
        for part in range(2):
            for block in range(blocks):
                piece = x_ref[r, part * half_depth:(part + 1) * half_depth, block * LANE:(block + 1) * LANE]
                piece = piece.astype(jnp.float32)
                sums = sums + piece * piece
    column[0:half_depth, :] = sums
    powers[me] = row_of(column[0:long_dates, :])

    pl.semaphore_wait(barrier, n - 1)

    def exchange(buffer, sems):
        def copy(k, slot):
            return pltpu.make_async_remote_copy(
                src_ref=buffer.at[slot], dst_ref=buffer.at[slot],
                send_sem=sems.at[0, k], recv_sem=sems.at[1, slot],
                device_id={"row": peer(k)}, device_id_type=MESH,
            )

        def start():
            @pl.loop(1, n)
            def _(k):
                copy(k, me).start()

        def finish():
            @pl.loop(1, n)
            def _(k):
                copy(k, peer(k)).wait_recv()

            @pl.loop(1, n)
            def _(k):
                copy(k, me).wait_send()

        return start, finish

    start_power, finish_power = exchange(powers, power_sem)
    start_ref, finish_ref = exchange(refs, ref_sem)
    start_power()

    def halo(t):
        up = pltpu.make_async_remote_copy(
            src_ref=x_ref.at[rows - t], dst_ref=low.at[HALF - t],
            send_sem=low_sem.at[0, t - 1], recv_sem=low_sem.at[1, t - 1],
            device_id={"row": jnp.minimum(me + 1, n - 1)}, device_id_type=MESH,
        )
        down = pltpu.make_async_remote_copy(
            src_ref=x_ref.at[t - 1], dst_ref=high.at[t - 1],
            send_sem=high_sem.at[0, t - 1], recv_sem=high_sem.at[1, t - 1],
            device_id={"row": jnp.maximum(me - 1, 0)}, device_id_type=MESH,
        )
        return up, down

    has_next = me < n - 1
    has_prev = me > 0
    for t in range(1, HALF + 1):
        up, down = halo(t)
        pl.when(has_next)(up.start)
        pl.when(has_prev)(down.start)

    @pl.when(me == 0)
    def _():
        low[...] = jnp.zeros_like(low)

    @pl.when(me == n - 1)
    def _():
        high[...] = jnp.zeros_like(high)

    row_ids = first_row + lax.broadcasted_iota(jnp.int32, (rows, cols), 0)
    col_ids = lax.broadcasted_iota(jnp.int32, (rows, cols), 1)
    chosen = []
    count = jnp.zeros((rows, cols), jnp.float32)
    for a in range(-HALF, HALF + 1):
        for b in range(-HALF, HALF + 1):
            inside = (row_ids + a >= 0) & (row_ids + a < total_rows)
            inside = inside & (col_ids + b >= 0) & (col_ids + b < cols)
            if (a, b) != (0, 0):
                inside = inside & (mask_ref[(a + HALF) * WIDTH + b + HALF] == 1)
            one = inside.astype(jnp.float32)
            chosen.append(one)
            count = count + one
    inverse = 1.0 / (count * ndate)

    def window(block):
        return max(0, block * LANE - SUB), min(cols, (block + 1) * LANE + SUB)

    coef[...] = jnp.zeros_like(coef)
    for block in range(blocks):
        begin, end = window(block)
        shape = (end - begin, LANE)
        shift = begin - block * LANE
        shift = shift + lax.broadcasted_iota(jnp.int32, shape, 0) - lax.broadcasted_iota(jnp.int32, shape, 1)
        for r in range(rows):
            for a in range(WIDTH):
                band = jnp.zeros(shape, jnp.float32)
                for b in range(WIDTH):
                    line = (chosen[a * WIDTH + b] * inverse)[r:r + 1, block * LANE:(block + 1) * LANE]
                    band = jnp.where(shift == b - HALF, line, band)
                weight[block, r, a, 0:end - begin, :] = band

    finish_power()
    power = jnp.sum(powers[...], axis=0)
    gain_row = lax.rsqrt(power * (1.0 / (total_rows * cols)) + 0.1)
    gain = jnp.broadcast_to(gain_row, (LANE, long_dates)).T[0:half_depth, :]
    gain = jnp.concatenate([gain] * blocks, axis=1)
    turned[...] = jnp.zeros_like(turned)

    def calibrate(source, place):
        for part in range(2):
            rows_here = slice(part * half_depth, (part + 1) * half_depth)
            scaled = (source[rows_here, :].astype(jnp.float32) * gain).astype(jnp.bfloat16)
            flat[rows_here, place * cols:(place + 1) * cols] = scaled
        turned[place] = flat[:, place * cols:(place + 1) * cols].T

    flat[...] = jnp.zeros_like(flat)
    def tile(r, block):
        start = (r + HALF) * cols + block * LANE
        return flat[0:half_depth, start:start + LANE], flat[half_depth:depth, start:start + LANE]

    def pair_of(real, imag):
        return jnp.concatenate(
            [jnp.concatenate([real, imag], axis=1), jnp.concatenate([imag, -real], axis=1)], axis=0
        )

    def project(r, block, a, pair):
        begin, end = window(block)
        proj = jnp.dot(turned[r + a, begin:end, 0:depth], pair, preferred_element_type=jnp.float32)
        band = weight[block, r, a, 0:end - begin, :]
        both = jnp.concatenate([band, band], axis=1)
        coef[block, a * cols + begin:a * cols + end, :] = (proj * both).astype(jnp.bfloat16)

    def update(r, block, first, last):
        return jnp.dot(
            flat[0:depth, (r + first) * cols:(r + last) * cols],
            coef[block, first * cols:last * cols, :], preferred_element_type=jnp.float32,
        )

    def partial_update(r, block, places):
        pair = pair_of(*tile(r, block))
        value = None
        for low_place, high_place in places:
            first, last = max(low_place - r, 0), min(high_place - r, WIDTH)
            if first >= last:
                continue
            for a in range(first, last):
                project(r, block, a, pair)
            term = update(r, block, first, last)
            value = term if value is None else value + term
        return value

    for r in range(rows):
        calibrate(x_ref.at[r], r + HALF)
    for r in range(rows):
        for block in range(blocks):
            total[r, block] = partial_update(r, block, [(HALF, HALF + rows)])

    def arrive(t):
        up, down = halo(t)
        pl.when(has_prev)(up.wait_recv)
        pl.when(has_next)(down.wait_recv)
        calibrate(low.at[HALF - t], HALF - t)
        calibrate(high.at[t - 1], HALF + rows + t - 1)

    def ring(t):
        return [(HALF - t, HALF - t + 1), (HALF + rows + t - 1, HALF + rows + t)]

    for t in range(1, HALF):
        arrive(t)
        for r in range(rows):
            for block in range(blocks):
                term = partial_update(r, block, ring(t))
                if term is not None:
                    total[r, block] += term
    arrive(HALF)

    target = index_ref[0]
    picked = jnp.zeros((depth, LANE), jnp.float32)
    for r in range(rows):
        for block in range(blocks):
            for step in range(ITERS):
                if step == 0:
                    product = total[r, block]
                    term = partial_update(r, block, ring(HALF))
                    if term is not None:
                        product = product + term
                else:
                    pair = pair_of(real, imag)
                    for a in range(WIDTH):
                        project(r, block, a, pair)
                    product = update(r, block, 0, WIDTH)
                top, bottom = product[0:half_depth], product[half_depth:depth]
                new_real = top[:, 0:LANE] - bottom[:, LANE:2 * LANE]
                new_imag = top[:, LANE:2 * LANE] + bottom[:, 0:LANE]
                energy = jnp.sum(new_real * new_real + new_imag * new_imag, axis=0, keepdims=True)
                factor = lax.rsqrt(energy * (1.0 / ndate) + 0.001)
                new_real = new_real * factor
                new_imag = new_imag * factor
                real = new_real.astype(jnp.bfloat16)
                imag = new_imag.astype(jnp.bfloat16)
            lanes = slice(block * LANE, (block + 1) * LANE)
            out_ref[r, 0:half_depth, lanes] = new_real
            out_ref[r, half_depth:depth, lanes] = new_imag
            place = (first_row + r) * cols + block * LANE + lax.broadcasted_iota(jnp.int32, (1, LANE), 1)
            here = place == target
            picked = picked + jnp.concatenate(
                [jnp.where(here, new_real, 0.0), jnp.where(here, new_imag, 0.0)], axis=0
            )

    column[...] = jnp.zeros_like(column)
    column[0:depth, :] = picked
    refs[me] = row_of(column[...])
    start_ref()
    finish_ref()
    refvec = jnp.sum(refs[...], axis=0)
    refvec = jnp.broadcast_to(refvec, (LANE, long_depth)).T
    ref_real = refvec[0:half_depth]
    ref_imag = refvec[half_depth:depth]
    for r in range(rows):
        for block in range(blocks):
            lanes = slice(block * LANE, (block + 1) * LANE)
            real = out_ref[r, 0:half_depth, lanes]
            imag = out_ref[r, half_depth:depth, lanes]
            out_ref[r, 0:half_depth, lanes] = real * ref_real + imag * ref_imag
            out_ref[r, half_depth:depth, lanes] = imag * ref_real - real * ref_imag

    for t in range(1, HALF + 1):
        up, down = halo(t)
        pl.when(has_next)(up.wait_send)
        pl.when(has_prev)(down.wait_send)


def per_device(slc, mask, ref_index):
    parts, ndate, rows, cols = slc.shape
    n = lax.axis_size("row")
    half_depth = round_up(ndate, SUB)
    depth = 2 * half_depth
    long_dates = round_up(half_depth, LANE)
    long_depth = round_up(depth, LANE)
    blocks = cols // LANE
    span = rows + 2 * HALF
    x = jnp.pad(slc.transpose(2, 0, 1, 3), ((0, 0), (0, 0), (0, half_depth - ndate), (0, 0)))
    x = x.reshape(rows, depth, cols)
    vmem = pl.BlockSpec(memory_space=pltpu.VMEM)

    def body(*refs):
        kernel(n, ndate, rows * n, *refs)

    out = pl.pallas_call(
        body,
        out_shape=jax.ShapeDtypeStruct((rows, depth, cols), jnp.float32),
        in_specs=[vmem, vmem, pl.BlockSpec(memory_space=pltpu.SMEM)],
        out_specs=vmem,
        scratch_shapes=[
            pltpu.VMEM((HALF, depth, cols), jnp.bfloat16),
            pltpu.VMEM((HALF, depth, cols), jnp.bfloat16),
            pltpu.VMEM((long_depth, span * cols), jnp.bfloat16),
            pltpu.VMEM((span, cols, long_depth), jnp.bfloat16),
            pltpu.VMEM((blocks, rows, WIDTH, LANE + 2 * SUB, LANE), jnp.float32),
            pltpu.VMEM((blocks, WIDTH * cols, 2 * LANE), jnp.bfloat16),
            pltpu.VMEM((rows, blocks, depth, 2 * LANE), jnp.float32),
            pltpu.VMEM((long_depth, LANE), jnp.float32),
            pltpu.VMEM((n, 1, long_dates), jnp.float32),
            pltpu.VMEM((n, 1, long_depth), jnp.float32),
            pltpu.SemaphoreType.DMA((2, HALF)),
            pltpu.SemaphoreType.DMA((2, HALF)),
            pltpu.SemaphoreType.DMA((2, n)),
            pltpu.SemaphoreType.DMA((2, n)),
        ],
        compiler_params=pltpu.CompilerParams(collective_id=0, has_side_effects=True),
        name="link",
    )(x, mask, ref_index)
    out = out.reshape(rows, parts, half_depth, cols)[:, :, :ndate]
    return out.transpose(1, 2, 0, 3)


def solution(mesh):
    placed = (P(None, None, ("grp", "row"), None), P(None, ("grp", "row"), None), P("grp"))
    return jax.shard_map(
        per_device,
        mesh=mesh,
        in_specs=placed,
        out_specs=P(None, None, ("grp", "row"), None),
        check_vma=False,
    )
```

```python
import jax
import jax.numpy as jnp
from jax import lax
from jax.experimental import pallas as pl
from jax.experimental.pallas import tpu as pltpu
from jax.sharding import PartitionSpec as P

HALF = 2
ITERS = 2
WIDTH = 2 * HALF + 1
LANE = 128
SUB = 16
MESH = pl.DeviceIdType.MESH


def round_up(value, unit):
    return (value + unit - 1) // unit * unit


def row_of(column_sums):
    return jnp.sum(column_sums.T, axis=0, keepdims=True)


def kernel(
    n, ndate, total_rows, x_ref, mask_ref, index_ref, out_ref,
    low, high, flat, turned, weight, coef, total, column, powers, refs,
    low_sem, high_sem, power_sem, ref_sem,
):
    rows, depth, cols = x_ref.shape
    half_depth = depth // 2
    blocks = cols // LANE
    long_dates = powers.shape[2]
    long_depth = refs.shape[2]
    me = lax.axis_index("row")
    first_row = me * rows

    def peer(k):
        return lax.rem(me + k, n)

    barrier = pltpu.get_barrier_semaphore()

    @pl.loop(1, n)
    def _(k):
        pl.semaphore_signal(barrier, inc=1, device_id={"row": peer(k)}, device_id_type=MESH)

    column[...] = jnp.zeros_like(column)
    sums = jnp.zeros((half_depth, LANE), jnp.float32)
    for r in range(rows):
        for part in range(2):
            for block in range(blocks):
                piece = x_ref[r, part * half_depth:(part + 1) * half_depth, block * LANE:(block + 1) * LANE]
                piece = piece.astype(jnp.float32)
                sums = sums + piece * piece
    column[0:half_depth, :] = sums
    powers[me] = row_of(column[0:long_dates, :])

    pl.semaphore_wait(barrier, n - 1)

    def exchange(buffer, sems):
        def copy(k, slot):
            return pltpu.make_async_remote_copy(
                src_ref=buffer.at[slot], dst_ref=buffer.at[slot],
                send_sem=sems.at[0, k], recv_sem=sems.at[1, slot],
                device_id={"row": peer(k)}, device_id_type=MESH,
            )

        def start():
            @pl.loop(1, n)
            def _(k):
                copy(k, me).start()

        def finish():
            @pl.loop(1, n)
            def _(k):
                copy(k, peer(k)).wait_recv()

            @pl.loop(1, n)
            def _(k):
                copy(k, me).wait_send()

        return start, finish

    start_power, finish_power = exchange(powers, power_sem)
    start_ref, finish_ref = exchange(refs, ref_sem)
    start_power()

    def halo(t):
        up = pltpu.make_async_remote_copy(
            src_ref=x_ref.at[rows - t], dst_ref=low.at[HALF - t],
            send_sem=low_sem.at[0, t - 1], recv_sem=low_sem.at[1, t - 1],
            device_id={"row": jnp.minimum(me + 1, n - 1)}, device_id_type=MESH,
        )
        down = pltpu.make_async_remote_copy(
            src_ref=x_ref.at[t - 1], dst_ref=high.at[t - 1],
            send_sem=high_sem.at[0, t - 1], recv_sem=high_sem.at[1, t - 1],
            device_id={"row": jnp.maximum(me - 1, 0)}, device_id_type=MESH,
        )
        return up, down

    has_next = me < n - 1
    has_prev = me > 0
    for t in range(1, HALF + 1):
        up, down = halo(t)
        pl.when(has_next)(up.start)
        pl.when(has_prev)(down.start)

    @pl.when(me == 0)
    def _():
        low[...] = jnp.zeros_like(low)

    @pl.when(me == n - 1)
    def _():
        high[...] = jnp.zeros_like(high)

    row_ids = first_row + lax.broadcasted_iota(jnp.int32, (rows, cols), 0)
    col_ids = lax.broadcasted_iota(jnp.int32, (rows, cols), 1)
    chosen = []
    count = jnp.zeros((rows, cols), jnp.float32)
    for a in range(-HALF, HALF + 1):
        for b in range(-HALF, HALF + 1):
            inside = (row_ids + a >= 0) & (row_ids + a < total_rows)
            inside = inside & (col_ids + b >= 0) & (col_ids + b < cols)
            if (a, b) != (0, 0):
                inside = inside & (mask_ref[(a + HALF) * WIDTH + b + HALF] == 1)
            one = inside.astype(jnp.float32)
            chosen.append(one)
            count = count + one
    inverse = 1.0 / (count * ndate)

    def window(block):
        return max(0, block * LANE - SUB), min(cols, (block + 1) * LANE + SUB)

    coef[...] = jnp.zeros_like(coef)
    for block in range(blocks):
        begin, end = window(block)
        shape = (end - begin, LANE)
        shift = begin - block * LANE
        shift = shift + lax.broadcasted_iota(jnp.int32, shape, 0) - lax.broadcasted_iota(jnp.int32, shape, 1)
        for r in range(rows):
            for a in range(WIDTH):
                band = jnp.zeros(shape, jnp.float32)
                for b in range(WIDTH):
                    line = (chosen[a * WIDTH + b] * inverse)[r:r + 1, block * LANE:(block + 1) * LANE]
                    band = jnp.where(shift == b - HALF, line, band)
                weight[block, r, a, 0:end - begin, :] = band

    flat[depth:, :] = jnp.zeros((flat.shape[0] - depth, flat.shape[1]), flat.dtype)
    finish_power()
    power = jnp.sum(powers[...], axis=0)
    gain_row = lax.rsqrt(power * (1.0 / (total_rows * cols)) + 0.1)
    gain = jnp.broadcast_to(gain_row, (LANE, long_dates)).T[0:half_depth, :]
    gain = jnp.concatenate([gain] * blocks, axis=1)

    def calibrate(source, place):
        for part in range(2):
            rows_here = slice(part * half_depth, (part + 1) * half_depth)
            scaled = (source[rows_here, :].astype(jnp.float32) * gain).astype(jnp.bfloat16)
            flat[rows_here, place * cols:(place + 1) * cols] = scaled
        turned[place] = flat[:, place * cols:(place + 1) * cols].T

    def tile(r, block):
        start = (r + HALF) * cols + block * LANE
        return flat[0:half_depth, start:start + LANE], flat[half_depth:depth, start:start + LANE]

    def pair_of(real, imag):
        return jnp.concatenate(
            [jnp.concatenate([real, imag], axis=1), jnp.concatenate([imag, -real], axis=1)], axis=0
        )

    def project(r, block, first, last, pair):
        begin, end = window(block)
        size = end - begin
        near = turned[r + first:r + last, begin:end, 0:depth].reshape((last - first) * size, depth)
        proj = jnp.dot(near, pair, preferred_element_type=jnp.float32)
        for a in range(first, last):
            band = weight[block, r, a, 0:size, :]
            both = jnp.concatenate([band, band], axis=1)
            piece = proj[(a - first) * size:(a - first + 1) * size]
            coef[block, a * cols + begin:a * cols + end, :] = (piece * both).astype(jnp.bfloat16)

    def update(r, block, first, last):
        return jnp.dot(
            flat[0:depth, (r + first) * cols:(r + last) * cols],
            coef[block, first * cols:last * cols, :], preferred_element_type=jnp.float32,
        )

    def partial_update(r, block, places):
        pair = pair_of(*tile(r, block))
        value = None
        for low_place, high_place in places:
            first, last = max(low_place - r, 0), min(high_place - r, WIDTH)
            if first >= last:
                continue
            project(r, block, first, last, pair)
            term = update(r, block, first, last)
            value = term if value is None else value + term
        return value

    for r in range(rows):
        calibrate(x_ref.at[r], r + HALF)
    for r in range(rows):
        for block in range(blocks):
            total[r, block] = partial_update(r, block, [(HALF, HALF + rows)])

    def arrive(t):
        up, down = halo(t)
        pl.when(has_prev)(up.wait_recv)
        pl.when(has_next)(down.wait_recv)
        calibrate(low.at[HALF - t], HALF - t)
        calibrate(high.at[t - 1], HALF + rows + t - 1)

    def ring(t):
        return [(HALF - t, HALF - t + 1), (HALF + rows + t - 1, HALF + rows + t)]

    for t in range(1, HALF):
        arrive(t)
        for r in range(rows):
            for block in range(blocks):
                term = partial_update(r, block, ring(t))
                if term is not None:
                    total[r, block] += term
    arrive(HALF)

    target = index_ref[0]
    picked = jnp.zeros((depth, LANE), jnp.float32)
    for r in range(rows):
        for block in range(blocks):
            for step in range(ITERS):
                if step == 0:
                    product = total[r, block]
                    term = partial_update(r, block, ring(HALF))
                    if term is not None:
                        product = product + term
                else:
                    pair = pair_of(real, imag)
                    project(r, block, 0, WIDTH, pair)
                    product = update(r, block, 0, WIDTH)
                top, bottom = product[0:half_depth], product[half_depth:depth]
                new_real = top[:, 0:LANE] - bottom[:, LANE:2 * LANE]
                new_imag = top[:, LANE:2 * LANE] + bottom[:, 0:LANE]
                energy = jnp.sum(new_real * new_real + new_imag * new_imag, axis=0, keepdims=True)
                factor = lax.rsqrt(energy * (1.0 / ndate) + 0.001)
                new_real = new_real * factor
                new_imag = new_imag * factor
                real = new_real.astype(jnp.bfloat16)
                imag = new_imag.astype(jnp.bfloat16)
            lanes = slice(block * LANE, (block + 1) * LANE)
            out_ref[r, 0:half_depth, lanes] = new_real
            out_ref[r, half_depth:depth, lanes] = new_imag
            place = (first_row + r) * cols + block * LANE + lax.broadcasted_iota(jnp.int32, (1, LANE), 1)
            here = place == target
            picked = picked + jnp.concatenate(
                [jnp.where(here, new_real, 0.0), jnp.where(here, new_imag, 0.0)], axis=0
            )

    column[...] = jnp.zeros_like(column)
    column[0:depth, :] = picked
    refs[me] = row_of(column[...])
    start_ref()
    finish_ref()
    refvec = jnp.sum(refs[...], axis=0)
    refvec = jnp.broadcast_to(refvec, (LANE, long_depth)).T
    ref_real = refvec[0:half_depth]
    ref_imag = refvec[half_depth:depth]
    for r in range(rows):
        for block in range(blocks):
            lanes = slice(block * LANE, (block + 1) * LANE)
            real = out_ref[r, 0:half_depth, lanes]
            imag = out_ref[r, half_depth:depth, lanes]
            out_ref[r, 0:half_depth, lanes] = real * ref_real + imag * ref_imag
            out_ref[r, half_depth:depth, lanes] = imag * ref_real - real * ref_imag

    for t in range(1, HALF + 1):
        up, down = halo(t)
        pl.when(has_next)(up.wait_send)
        pl.when(has_prev)(down.wait_send)


def per_device(slc, mask, ref_index):
    parts, ndate, rows, cols = slc.shape
    n = lax.axis_size("row")
    half_depth = round_up(ndate, SUB)
    depth = 2 * half_depth
    long_dates = round_up(half_depth, LANE)
    long_depth = round_up(depth, LANE)
    blocks = cols // LANE
    span = rows + 2 * HALF
    x = jnp.pad(slc.transpose(2, 0, 1, 3), ((0, 0), (0, 0), (0, half_depth - ndate), (0, 0)))
    x = x.reshape(rows, depth, cols)
    vmem = pl.BlockSpec(memory_space=pltpu.VMEM)

    def body(*refs):
        kernel(n, ndate, rows * n, *refs)

    out = pl.pallas_call(
        body,
        out_shape=jax.ShapeDtypeStruct((rows, depth, cols), jnp.float32),
        in_specs=[vmem, vmem, pl.BlockSpec(memory_space=pltpu.SMEM)],
        out_specs=vmem,
        scratch_shapes=[
            pltpu.VMEM((HALF, depth, cols), jnp.bfloat16),
            pltpu.VMEM((HALF, depth, cols), jnp.bfloat16),
            pltpu.VMEM((long_depth, span * cols), jnp.bfloat16),
            pltpu.VMEM((span, cols, long_depth), jnp.bfloat16),
            pltpu.VMEM((blocks, rows, WIDTH, LANE + 2 * SUB, LANE), jnp.float32),
            pltpu.VMEM((blocks, WIDTH * cols, 2 * LANE), jnp.bfloat16),
            pltpu.VMEM((rows, blocks, depth, 2 * LANE), jnp.float32),
            pltpu.VMEM((long_depth, LANE), jnp.float32),
            pltpu.VMEM((n, 1, long_dates), jnp.float32),
            pltpu.VMEM((n, 1, long_depth), jnp.float32),
            pltpu.SemaphoreType.DMA((2, HALF)),
            pltpu.SemaphoreType.DMA((2, HALF)),
            pltpu.SemaphoreType.DMA((2, n)),
            pltpu.SemaphoreType.DMA((2, n)),
        ],
        compiler_params=pltpu.CompilerParams(collective_id=0, has_side_effects=True),
        name="link",
    )(x, mask, ref_index)
    out = out.reshape(rows, parts, half_depth, cols)[:, :, :ndate]
    return out.transpose(1, 2, 0, 3)


def solution(mesh):
    placed = (P(None, None, ("grp", "row"), None), P(None, ("grp", "row"), None), P("grp"))
    return jax.shard_map(
        per_device,
        mesh=mesh,
        in_specs=placed,
        out_specs=P(None, None, ("grp", "row"), None),
        check_vma=False,
    )
```

```python
import jax
import jax.numpy as jnp
from jax import lax
from jax.experimental import pallas as pl
from jax.experimental.pallas import tpu as pltpu
from jax.sharding import PartitionSpec as P

HALF = 2
ITERS = 2
WIDTH = 2 * HALF + 1
LANE = 128
SUB = 16
MESH = pl.DeviceIdType.MESH


def round_up(value, unit):
    return (value + unit - 1) // unit * unit


def row_of(column_sums):
    return jnp.sum(column_sums.T, axis=0, keepdims=True)


def kernel(
    n, ndate, total_rows, x_ref, mask_ref, index_ref, out_ref,
    low, high, flat, turned, weight, coef, total, column, powers, refs,
    low_sem, high_sem, power_sem, ref_sem,
):
    rows, depth, cols = x_ref.shape
    half_depth = depth // 2
    blocks = cols // LANE
    long_dates = powers.shape[2]
    long_depth = refs.shape[2]
    me = lax.axis_index("row")
    first_row = me * rows

    def peer(k):
        return lax.rem(me + k, n)

    barrier = pltpu.get_barrier_semaphore()

    @pl.loop(1, n)
    def _(k):
        pl.semaphore_signal(barrier, inc=1, device_id={"row": peer(k)}, device_id_type=MESH)

    column[...] = jnp.zeros_like(column)
    sums = jnp.zeros((half_depth, LANE), jnp.float32)
    for r in range(rows):
        for part in range(2):
            for block in range(blocks):
                piece = x_ref[r, part * half_depth:(part + 1) * half_depth, block * LANE:(block + 1) * LANE]
                piece = piece.astype(jnp.float32)
                sums = sums + piece * piece
    column[0:half_depth, :] = sums
    powers[me] = row_of(column[0:long_dates, :])

    pl.semaphore_wait(barrier, n - 1)

    def exchange(buffer, sems):
        def copy(k, slot):
            return pltpu.make_async_remote_copy(
                src_ref=buffer.at[slot], dst_ref=buffer.at[slot],
                send_sem=sems.at[0, k], recv_sem=sems.at[1, slot],
                device_id={"row": peer(k)}, device_id_type=MESH,
            )

        def start():
            @pl.loop(1, n)
            def _(k):
                copy(k, me).start()

        def finish():
            @pl.loop(1, n)
            def _(k):
                copy(k, peer(k)).wait_recv()

            @pl.loop(1, n)
            def _(k):
                copy(k, me).wait_send()

        return start, finish

    start_power, finish_power = exchange(powers, power_sem)
    start_ref, finish_ref = exchange(refs, ref_sem)
    start_power()

    def halo(t):
        up = pltpu.make_async_remote_copy(
            src_ref=x_ref.at[rows - t], dst_ref=low.at[HALF - t],
            send_sem=low_sem.at[0, t - 1], recv_sem=low_sem.at[1, t - 1],
            device_id={"row": jnp.minimum(me + 1, n - 1)}, device_id_type=MESH,
        )
        down = pltpu.make_async_remote_copy(
            src_ref=x_ref.at[t - 1], dst_ref=high.at[t - 1],
            send_sem=high_sem.at[0, t - 1], recv_sem=high_sem.at[1, t - 1],
            device_id={"row": jnp.maximum(me - 1, 0)}, device_id_type=MESH,
        )
        return up, down

    has_next = me < n - 1
    has_prev = me > 0
    for t in range(1, HALF + 1):
        up, down = halo(t)
        pl.when(has_next)(up.start)
        pl.when(has_prev)(down.start)

    @pl.when(me == 0)
    def _():
        low[...] = jnp.zeros_like(low)

    @pl.when(me == n - 1)
    def _():
        high[...] = jnp.zeros_like(high)

    row_ids = first_row + lax.broadcasted_iota(jnp.int32, (rows, cols), 0)
    col_ids = lax.broadcasted_iota(jnp.int32, (rows, cols), 1)
    chosen = []
    count = jnp.zeros((rows, cols), jnp.float32)
    for a in range(-HALF, HALF + 1):
        for b in range(-HALF, HALF + 1):
            inside = (row_ids + a >= 0) & (row_ids + a < total_rows)
            inside = inside & (col_ids + b >= 0) & (col_ids + b < cols)
            if (a, b) != (0, 0):
                inside = inside & (mask_ref[(a + HALF) * WIDTH + b + HALF] == 1)
            one = inside.astype(jnp.float32)
            chosen.append(one)
            count = count + one
    inverse = 1.0 / (count * ndate)

    def window(block):
        return max(0, block * LANE - SUB), min(cols, (block + 1) * LANE + SUB)

    coef[...] = jnp.zeros_like(coef)
    for block in range(blocks):
        begin, end = window(block)
        shape = (end - begin, LANE)
        shift = begin - block * LANE
        shift = shift + lax.broadcasted_iota(jnp.int32, shape, 0) - lax.broadcasted_iota(jnp.int32, shape, 1)
        for r in range(rows):
            for a in range(WIDTH):
                band = jnp.zeros(shape, jnp.float32)
                for b in range(WIDTH):
                    line = (chosen[a * WIDTH + b] * inverse)[r:r + 1, block * LANE:(block + 1) * LANE]
                    band = jnp.where(shift == b - HALF, line, band)
                weight[block, r, a, 0:end - begin, :] = band

    flat[depth:, :] = jnp.zeros((flat.shape[0] - depth, flat.shape[1]), flat.dtype)
    finish_power()
    power = jnp.sum(powers[...], axis=0)
    gain_row = lax.rsqrt(power * (1.0 / (total_rows * cols)) + 0.1)
    gain = jnp.broadcast_to(gain_row, (LANE, long_dates)).T[0:half_depth, :]
    gain = jnp.concatenate([gain] * blocks, axis=1)

    def calibrate(source, place):
        for part in range(2):
            rows_here = slice(part * half_depth, (part + 1) * half_depth)
            scaled = (source[rows_here, :].astype(jnp.float32) * gain).astype(jnp.bfloat16)
            flat[rows_here, place * cols:(place + 1) * cols] = scaled
        turned[place] = flat[:, place * cols:(place + 1) * cols].T

    def tile(r, block):
        start = (r + HALF) * cols + block * LANE
        return flat[0:half_depth, start:start + LANE], flat[half_depth:depth, start:start + LANE]

    def pair_of(real, imag):
        return jnp.concatenate(
            [jnp.concatenate([real, imag], axis=1), jnp.concatenate([imag, -real], axis=1)], axis=0
        )

    def project(r, block, a, pair):
        begin, end = window(block)
        proj = jnp.dot(turned[r + a, begin:end, 0:depth], pair, preferred_element_type=jnp.float32)
        band = weight[block, r, a, 0:end - begin, :]
        both = jnp.concatenate([band, band], axis=1)
        coef[block, a * cols + begin:a * cols + end, :] = (proj * both).astype(jnp.bfloat16)

    def update(r, block, first, last):
        return jnp.dot(
            flat[0:depth, (r + first) * cols:(r + last) * cols],
            coef[block, first * cols:last * cols, :], preferred_element_type=jnp.float32,
        )

    def partial_update(r, block, places):
        pair = pair_of(*tile(r, block))
        value = None
        for low_place, high_place in places:
            first, last = max(low_place - r, 0), min(high_place - r, WIDTH)
            if first >= last:
                continue
            for a in range(first, last):
                project(r, block, a, pair)
            term = update(r, block, first, last)
            value = term if value is None else value + term
        return value

    for r in range(rows):
        calibrate(x_ref.at[r], r + HALF)
    for r in range(rows):
        for block in range(blocks):
            total[r, block] = partial_update(r, block, [(HALF, HALF + rows)])

    def arrive(t):
        up, down = halo(t)
        pl.when(has_prev)(up.wait_recv)
        pl.when(has_next)(down.wait_recv)
        calibrate(low.at[HALF - t], HALF - t)
        calibrate(high.at[t - 1], HALF + rows + t - 1)

    def ring(t):
        return [(HALF - t, HALF - t + 1), (HALF + rows + t - 1, HALF + rows + t)]

    for t in range(1, HALF):
        arrive(t)
        for r in range(rows):
            for block in range(blocks):
                term = partial_update(r, block, ring(t))
                if term is not None:
                    total[r, block] += term
    arrive(HALF)

    target = index_ref[0]
    picked = jnp.zeros((depth, LANE), jnp.float32)
    for r in range(rows):
        for block in range(blocks):
            for step in range(ITERS):
                if step == 0:
                    product = total[r, block]
                    term = partial_update(r, block, ring(HALF))
                    if term is not None:
                        product = product + term
                else:
                    pair = pair_of(real, imag)
                    for a in range(WIDTH):
                        project(r, block, a, pair)
                    product = update(r, block, 0, WIDTH)
                top, bottom = product[0:half_depth], product[half_depth:depth]
                new_real = top[:, 0:LANE] - bottom[:, LANE:2 * LANE]
                new_imag = top[:, LANE:2 * LANE] + bottom[:, 0:LANE]
                energy = jnp.sum(new_real * new_real + new_imag * new_imag, axis=0, keepdims=True)
                factor = lax.rsqrt(energy * (1.0 / ndate) + 0.001)
                new_real = new_real * factor
                new_imag = new_imag * factor
                real = new_real.astype(jnp.bfloat16)
                imag = new_imag.astype(jnp.bfloat16)
            lanes = slice(block * LANE, (block + 1) * LANE)
            out_ref[r, 0:half_depth, lanes] = new_real
            out_ref[r, half_depth:depth, lanes] = new_imag
            place = (first_row + r) * cols + block * LANE + lax.broadcasted_iota(jnp.int32, (1, LANE), 1)
            here = place == target
            picked = picked + jnp.concatenate(
                [jnp.where(here, new_real, 0.0), jnp.where(here, new_imag, 0.0)], axis=0
            )

    column[...] = jnp.zeros_like(column)
    column[0:depth, :] = picked
    refs[me] = row_of(column[...])
    start_ref()
    finish_ref()
    refvec = jnp.sum(refs[...], axis=0)
    refvec = jnp.broadcast_to(refvec, (LANE, long_depth)).T
    ref_real = refvec[0:half_depth]
    ref_imag = refvec[half_depth:depth]
    for r in range(rows):
        for block in range(blocks):
            lanes = slice(block * LANE, (block + 1) * LANE)
            real = out_ref[r, 0:half_depth, lanes]
            imag = out_ref[r, half_depth:depth, lanes]
            out_ref[r, 0:half_depth, lanes] = real * ref_real + imag * ref_imag
            out_ref[r, half_depth:depth, lanes] = imag * ref_real - real * ref_imag

    for t in range(1, HALF + 1):
        up, down = halo(t)
        pl.when(has_next)(up.wait_send)
        pl.when(has_prev)(down.wait_send)


def per_device(slc, mask, ref_index):
    parts, ndate, rows, cols = slc.shape
    n = lax.axis_size("row")
    half_depth = round_up(ndate, SUB)
    depth = 2 * half_depth
    long_dates = round_up(half_depth, LANE)
    long_depth = round_up(depth, LANE)
    blocks = cols // LANE
    span = rows + 2 * HALF
    x = jnp.pad(slc.transpose(2, 0, 1, 3), ((0, 0), (0, 0), (0, half_depth - ndate), (0, 0)))
    x = x.reshape(rows, depth, cols)
    vmem = pl.BlockSpec(memory_space=pltpu.VMEM)

    def body(*refs):
        kernel(n, ndate, rows * n, *refs)

    out = pl.pallas_call(
        body,
        out_shape=jax.ShapeDtypeStruct((rows, depth, cols), jnp.float32),
        in_specs=[vmem, vmem, pl.BlockSpec(memory_space=pltpu.SMEM)],
        out_specs=vmem,
        scratch_shapes=[
            pltpu.VMEM((HALF, depth, cols), jnp.bfloat16),
            pltpu.VMEM((HALF, depth, cols), jnp.bfloat16),
            pltpu.VMEM((long_depth, span * cols), jnp.bfloat16),
            pltpu.VMEM((span, cols, long_depth), jnp.bfloat16),
            pltpu.VMEM((blocks, rows, WIDTH, LANE + 2 * SUB, LANE), jnp.float32),
            pltpu.VMEM((blocks, WIDTH * cols, 2 * LANE), jnp.bfloat16),
            pltpu.VMEM((rows, blocks, depth, 2 * LANE), jnp.float32),
            pltpu.VMEM((long_depth, LANE), jnp.float32),
            pltpu.VMEM((n, 1, long_dates), jnp.float32),
            pltpu.VMEM((n, 1, long_depth), jnp.float32),
            pltpu.SemaphoreType.DMA((2, HALF)),
            pltpu.SemaphoreType.DMA((2, HALF)),
            pltpu.SemaphoreType.DMA((2, n)),
            pltpu.SemaphoreType.DMA((2, n)),
        ],
        compiler_params=pltpu.CompilerParams(collective_id=0, has_side_effects=True),
        name="link",
    )(x, mask, ref_index)
    out = out.reshape(rows, parts, half_depth, cols)[:, :, :ndate]
    return out.transpose(1, 2, 0, 3)


def solution(mesh):
    placed = (P(None, None, ("grp", "row"), None), P(None, ("grp", "row"), None), P("grp"))
    return jax.shard_map(
        per_device,
        mesh=mesh,
        in_specs=placed,
        out_specs=P(None, None, ("grp", "row"), None),
        check_vma=False,
    )
```
